32 devices in a mesh: lat: 4 (over x, core), ch: 8 (over z, y).
Axes of the slice: x: 2, y: 2, z: 4, core: 2. Of those that a mesh axis runs over, the one named last changes fastest.
Arguments:
- field: bfloat16 [256, 1024, 2048], P('ch', 'lat'), may hold values from -6 to 6
- band: float32 [2, 5, 1024], replicated, may hold values from -1 to 1
- mixing: bfloat16 [2, 256, 256], replicated, may hold values from -0.375 to 0.375
Outputs:
- filtered: bfloat16 [256, 1024, 2048], P('ch', 'lat')
The draws below stay inside these ranges and needn't reach their ends.
All inputs are finite; a program needn't handle non-finite values.
Results may differ from the reference program's by a relative error of at most 0.0092.
Values may be sent and summed in bfloat16 or wider, within the bound.
A program may use at most 256 MiB of HBM per device.

```python
import math
import jax
import jax.numpy as jnp
from jax import lax

C = 256
NLAT = 1024
NLON = 2048
KM = 512
KL = 1024


def steps_of(key, shape, pieces, smallest, largest):
    def one(position, shards_of):
        steps = jax.random.uniform(jax.random.fold_in(jax.random.fold_in(key, 6), position), (shards_of,), jnp.float32, smallest / len(pieces), largest / len(pieces))
        return jnp.repeat(jnp.exp(steps), shape[position] // shards_of).reshape((-1,) + (1,) * (len(shape) - position - 1))

    loudness = one(*pieces[0])
    for cut in pieces[1:]:
        loudness = loudness * one(*cut)
    return loudness


def noise(rng, shape, spread, limit, pieces=(), held_as=jnp.bfloat16):
    gain = steps_of(rng, shape, pieces, -0.22, 0.18) if pieces else 1.0
    entries = jax.random.normal(rng, shape, jnp.float32) * spread * gain
    return jnp.minimum(jnp.maximum(entries, -limit), limit).astype(held_as)


def setup_inputs(seed: int = 0) -> dict:
    key_list = jax.random.split(jax.random.key(seed), 4)
    field = noise(key_list[0], (C, NLAT, NLON), 1.0, 6.0, ((0, 8), (1, 4)))
    band = jnp.clip(jax.random.uniform(key_list[1], (2, 5, KL), jnp.float32, -1.0, 1.0), -1.0, 1.0)
    mixing = noise(key_list[2], (2, C, C), C ** -0.5, 0.375)
    return {"field": field, "band": band, "mixing": mixing}


def lon_wave(column, points):
    parity = column // KM
    component = column % KM // (KM // 2)
    longitude_mode = 2 * (column % (KM // 2)) + parity
    phase_angles = points[:, None] * longitude_mode[None, :] % NLON
    angles = phase_angles.astype(jnp.float32) * (2.0 * math.pi / NLON)
    wave_table = jnp.where(component[None, :] == 0, jnp.cos(angles), jnp.sin(angles)) / math.sqrt(NLON)
    weight = jnp.where(longitude_mode == 0, 1.0, 2.0).astype(jnp.float32)
    return (wave_table, weight)

def lat_table(parity):
    index_of_row = jnp.arange(NLAT, dtype=jnp.int32)
    wavenumbers = jnp.arange(KL, dtype=jnp.int32) + parity
    phase_angles = (2 * index_of_row[:, None] + 1) * wavenumbers[None, :] % (4 * NLAT)
    angles = phase_angles.astype(jnp.float32) * (math.pi / (2 * NLAT))
    wave_table = jnp.where(parity == 0, jnp.cos(angles), jnp.sin(angles))
    return (wave_table * math.sqrt(2.0 / NLAT)).astype(jnp.bfloat16)

def convert(amplitudes, coeffs):
    padded = jnp.pad(amplitudes, ((2, 2), (0, 0)))
    summed = coeffs[0][:, None] * padded[0:KL]
    for offset in range(1, 5):
        summed = summed + coeffs[offset][:, None] * padded[offset:offset + KL]
    return summed

def reference(field, band, mixing):
    column_all = jnp.arange(2 * KM, dtype=jnp.int32)
    points = jnp.arange(NLON, dtype=jnp.int32)
    wave_table, weight = lon_wave(column_all, points)
    forward_lon = wave_table.astype(jnp.bfloat16)
    longitude_inverse_transform = (wave_table * weight[None, :]).T.astype(jnp.bfloat16)

    def longitude_forward_transform(plane):
        return jnp.dot(plane, forward_lon, preferred_element_type=jnp.float32).astype(jnp.bfloat16)
    spectra = lax.map(longitude_forward_transform, field)
    halves = []
    for parity in range(2):
        legendre_table = lat_table(parity)
        part_spectra = spectra[:, :, parity * KM:(parity + 1) * KM]
        coeffs = band[parity]

        def forward_part(plane):
            amplitudes = jnp.dot(legendre_table.T, plane, preferred_element_type=jnp.float32)
            return convert(amplitudes, coeffs).astype(jnp.bfloat16)
        converted = lax.map(forward_part, part_spectra)
        mixed = jnp.dot(mixing[parity], converted.reshape(C, KL * KM), preferred_element_type=jnp.float32)
        mixed = mixed.astype(jnp.bfloat16).reshape(C, KL, KM)

        def inverse_part(plane):
            return jnp.dot(legendre_table, plane, preferred_element_type=jnp.float32).astype(jnp.bfloat16)
        halves.append(lax.map(inverse_part, mixed))
    lat_rows = jnp.concatenate(halves, axis=2)

    def lon_inverse(plane):
        return jnp.dot(plane, longitude_inverse_transform, preferred_element_type=jnp.float32).astype(jnp.bfloat16)
    return lax.map(lon_inverse, lat_rows)
```

```python
import functools
import math

import jax
import jax.numpy as jnp
import numpy as np
from jax import lax
from jax.experimental import pallas as pl
from jax.experimental.pallas import tpu as pltpu
from jax.sharding import PartitionSpec as P

AXES = ("lat", "ch")
CHUNKS = 2


def lon_half(cols, nlon):
    km = cols // 2
    column = np.arange(cols)
    mode = 2 * (column % (km // 2)) + column // km
    phase = (np.arange(nlon // 2)[:, None] * mode[None, :] % nlon) * (2.0 * math.pi / nlon)
    cosine = (column % km // (km // 2) == 0)[None, :]
    table = np.where(cosine, np.cos(phase), np.sin(phase)) / math.sqrt(nlon)
    return table.astype(jnp.bfloat16), np.where(mode == 0, 1.0, 2.0).astype(jnp.bfloat16)


def lat_table(parity, nlat, kl):
    rows = jnp.arange(nlat, dtype=jnp.int32)
    waves = jnp.arange(kl, dtype=jnp.int32) + parity
    angles = ((2 * rows[:, None] + 1) * waves[None, :] % (4 * nlat)).astype(jnp.float32)
    angles = angles * (math.pi / (2 * nlat))
    table = jnp.where(parity == 0, jnp.cos(angles), jnp.sin(angles))
    return (table * math.sqrt(2.0 / nlat)).astype(jnp.bfloat16)


def lon_inverse_kernel(chunks, *refs):
    blocks, table, out = refs[:chunks], refs[chunks], refs[chunks + 1]
    nd, _, kc, rows = blocks[0].shape
    half = out.shape[2] // 2
    sums = []
    for p in range(2):
        total = None
        for j in range(chunks):
            x = blocks[j][p * (nd // 2) : (p + 1) * (nd // 2), 0].reshape(nd // 2 * kc, rows)
            part = lax.dot_general(
                x, table[j, p], (((0,), (0,)), ((), ())), preferred_element_type=jnp.float32
            )
            total = part if total is None else total + part
        sums.append(total)
    out[0, :, :half] = (sums[0] + sums[1]).astype(out.dtype)
    out[0, :, half:] = (sums[0] - sums[1]).astype(out.dtype)


def lon_inverse(back, inverse, nlon):
    chunks = len(back)
    nd, c, kc, rows = back[0].shape
    table = inverse.reshape(nlon // 2, 2, nd // 2, chunks, kc).transpose(3, 1, 2, 4, 0)
    table = table.reshape(chunks, 2, nd // 2 * kc, nlon // 2)
    if kc % 16 == 0:
        return pl.pallas_call(
            functools.partial(lon_inverse_kernel, chunks),
            grid=(c,),
            in_specs=[pl.BlockSpec((nd, 1, kc, rows), lambda i: (0, i, 0, 0))] * chunks
            + [pl.BlockSpec(table.shape, lambda i: (0, 0, 0, 0))],
            out_specs=pl.BlockSpec((1, rows, nlon), lambda i: (i, 0, 0)),
            out_shape=jax.ShapeDtypeStruct((c, rows, nlon), jnp.bfloat16),
            compiler_params=pltpu.CompilerParams(vmem_limit_bytes=48 << 20),
            cost_estimate=pl.CostEstimate(
                flops=2 * c * rows * nlon * nd * kc * chunks // 2,
                bytes_accessed=2 * c * rows * (nlon + nd * kc * chunks),
                transcendentals=0,
            ),
        )(*back, table)
    x = jnp.stack(back).reshape(chunks, 2, nd // 2, c, kc, rows)
    t = table.reshape(chunks, 2, nd // 2, kc, nlon // 2)
    even, odd = (
        jnp.einsum("jdckr,jdkn->crn", x[:, p], t[:, p], preferred_element_type=jnp.float32) for p in range(2)
    )
    return jnp.concatenate([even + odd, even - odd], 2).astype(jnp.bfloat16)


def per_device(field, band, mixing):
    nl, nc = lax.axis_size("lat"), lax.axis_size("ch")
    nd = nl * nc
    c, rows, nlon = field.shape
    nlat, kl = rows * nl, band.shape[2]
    cols = nlon // 2
    km = cols // 2
    share = cols // nd
    chunks = CHUNKS if share % CHUNKS == 0 else 1
    kc = share // chunks
    me = lax.axis_index("lat") * nc + lax.axis_index("ch")
    parity = me * share // km

    half, weight = lon_half(cols, nlon)
    half = jnp.asarray(half)
    sign = jnp.where(jnp.arange(cols) < km, 1.0, -1.0).astype(jnp.bfloat16)
    forward = jnp.concatenate([half, half * sign], 0).reshape(nlon, nd, chunks, kc)

    sent = []
    for j in range(chunks):
        spectra = jnp.einsum("crn,ndk->dkcr", field, forward[:, :, j], preferred_element_type=jnp.float32)
        sent.append(lax.all_to_all(spectra.astype(jnp.bfloat16), AXES, 0, 0, tiled=True))

    table = lat_table(parity, nlat, kl)
    coeffs = lax.dynamic_index_in_dim(band, parity, 0, keepdims=False)
    weights = lax.dynamic_index_in_dim(mixing, parity, 0, keepdims=False)
    padded = jnp.pad(table.astype(jnp.float32), ((0, 0), (2, 2)))
    conv = sum(coeffs[s][None, :] * padded[:, s : s + kl] for s in range(5))
    kernel = jnp.einsum("rl,ql->rq", conv.astype(jnp.bfloat16), table, preferred_element_type=jnp.float32)
    kernel = kernel.astype(jnp.bfloat16).reshape(nl, rows, nl, rows)

    back = []
    for j in range(chunks):
        got = sent[j].reshape(nl, nc, kc, c, rows)
        w = weights.reshape(nc * c, nc, c)
        mixed = jnp.einsum("ojc,ijkcr->kior", w, got, preferred_element_type=jnp.float32).astype(jnp.bfloat16)
        z = jnp.einsum("kior,irsq->skoq", mixed, kernel, preferred_element_type=jnp.float32).astype(jnp.bfloat16)
        z = z.reshape(nl, kc, nc, c, rows).transpose(0, 2, 3, 1, 4).reshape(nd, c, kc, rows)
        back.append(lax.all_to_all(z, AXES, 0, 0, tiled=True))
    return lon_inverse(back, half * jnp.asarray(weight), nlon)


def solution(mesh):
    return jax.shard_map(
        per_device,
        mesh=mesh,
        in_specs=(P("ch", "lat", None), P(), P()),
        out_specs=P("ch", "lat", None),
        check_vma=False,
    )
```
